32 devices in a mesh: grp: 2 (over y), ia: 4 (over z), ja: 4 (over x, core).
Axes of the slice: x: 2, y: 2, z: 4, core: 2. Of those that a mesh axis runs over, the one named last changes fastest.
Arguments:
- doubles: bfloat16 [8, 16, 384, 384], P(('grp', 'ia'), 'ja'), parts along dimension 0, may hold values from -6 to 6
- aux_factors: bfloat16 [4, 384, 384], P('ia'), may hold values from -0.15625 to 0.15625
- cycle_factors: bfloat16 [16, 384, 128], replicated, may hold values from -0.21875 to 0.21875
Outputs:
- sigma: bfloat16 [8, 16, 384, 384], P(('grp', 'ia'), 'ja'), parts along dimension 0
The draws below stay inside these ranges and needn't reach their ends.
There are 2 independent parts, one for each index of `grp`. The reference program is written for one: setup_inputs(seed, part) draws one part's arguments, and reference() takes and returns one part's arrays. A program takes and returns all parts, laid end to end along the dimension named above; an argument that names none is the same for every part. Nothing has to cross between parts.
All inputs are finite; a program needn't handle non-finite values.
Results may differ from the reference program's by a relative error of at most 0.008.
Values may be sent and summed in bfloat16 or wider, within the bound.
No kernel may reach another device: no remote copies, remote signals or barrier semaphores. Data moves between devices by JAX's collectives and lax.ppermute only.
A program may use at most 128 MiB of HBM per device.

```python
import jax
import jax.numpy as jnp
from jax import lax

V = 384
Q = 128
AUX = 4
OI = 4
J_ALL = 16


def block_scale(rng, dims, split, low, high):
    loudness = 1.0
    for dim, shards_of in split:
        draws = jax.random.uniform(jax.random.fold_in(jax.random.fold_in(rng, 6), dim), (shards_of,), jnp.float32, low / len(split), high / len(split))
        loudness = loudness * jnp.repeat(jnp.exp(draws), dims[dim] // shards_of).reshape((-1,) + (1,) * (len(dims) - 1 - dim))
    return loudness


def noise(own_key, dims, spread, reach, shards=(), held_as=jnp.bfloat16):
    result = jax.random.normal(own_key, dims, jnp.float32) * spread
    if len(shards) > 0:
        result = block_scale(own_key, dims, shards, -0.22, 0.18) * result
    return jnp.clip(result, min=-reach, max=reach).astype(held_as)


def setup_inputs(seed: int = 0, part: int = 0) -> dict:
    streams_of = jax.random.split(jax.random.key(seed), 4)
    own_keys = jax.random.split(jax.random.fold_in(streams_of[3], part), 4)
    doubles = noise(own_keys[0], (OI, J_ALL, V, V), 1.0, 6.0, ((0, 4), (1, 4)))
    aux_factors = noise(streams_of[1], (AUX, V, V), (V * 4) ** -0.5, 0.15625, ((0, 4),))
    cycle_factors = noise(streams_of[2], (J_ALL, V, Q), (J_ALL * V // 8) ** -0.5, 0.21875)
    return dict(doubles=doubles, aux_factors=aux_factors, cycle_factors=cycle_factors)


def ladder_terms(pair_blocks, factor):
    wide_pairs = pair_blocks.astype(jnp.float32)
    wide_factor = factor.astype(jnp.float32)
    halfway = jnp.einsum('pcd,bd->pcb', wide_pairs, wide_factor).astype(jnp.bfloat16)
    return jnp.einsum('ac,pcb->pab', wide_factor, halfway.astype(jnp.float32))


def reference(doubles, aux_factors, cycle_factors):
    pair_blocks = doubles.reshape(OI * J_ALL, V, V)

    def one_step(position, running):
        factor = lax.dynamic_index_in_dim(aux_factors, position, 0, keepdims=False)
        return running + ladder_terms(pair_blocks, factor)

    ladder = lax.fori_loop(0, AUX, one_step, jnp.zeros((OI * J_ALL, V, V), jnp.float32))
    ladder = ladder.reshape(OI, J_ALL, V, V)
    wide_cycle = cycle_factors.astype(jnp.float32)
    latent = jnp.einsum('ijab,jbq->iaq', doubles.astype(jnp.float32), wide_cycle).astype(jnp.bfloat16)
    cycle_term = jnp.einsum('iaq,jbq->ijab', latent.astype(jnp.float32), wide_cycle).astype(jnp.bfloat16)
    return (ladder + cycle_term.astype(jnp.float32)).astype(jnp.bfloat16)
```

```python
import functools

import jax
import jax.numpy as jnp
from jax import lax
from jax.experimental import pallas as pl
from jax.experimental.pallas import tpu as pltpu
from jax.sharding import PartitionSpec as P

F32 = jnp.float32
BF16 = jnp.bfloat16
NT = (((1,), (1,)), ((), ()))
VMEM = pl.BlockSpec(memory_space=pltpu.VMEM)
HBM = pl.BlockSpec(memory_space=pltpu.HBM)


def call(kernel, outs, specs, scratch=(), aliases=None, flops=0, moved=0, name=None):
    return pl.pallas_call(
        kernel,
        out_shape=outs,
        in_specs=specs,
        out_specs=jax.tree.map(lambda o: VMEM if isinstance(o, pl.MemoryRef) else HBM, outs),
        scratch_shapes=scratch,
        input_output_aliases=aliases or {},
        cost_estimate=pl.CostEstimate(flops=flops, bytes_accessed=moved, transcendentals=0),
        compiler_params=pltpu.CompilerParams(vmem_limit_bytes=24 << 20),
        name=name,
    )


def mm(a, b):
    return jnp.dot(a, b, preferred_element_type=F32)


def mm_nt(a, b):
    return lax.dot_general(a, b, NT, preferred_element_type=F32)


def take_rows(rows, index_of, src, out, sem):
    start = pl.multiple_of(index_of() * rows, rows)
    copy = pltpu.make_async_copy(src.at[pl.ds(start, rows), :], out, sem)
    copy.start()
    copy.wait()


def latent_part(core_of, first_j, r, u_all, keep, send, u, total, sem):
    n = r.shape[0]
    copy = pltpu.make_async_copy(u_all.at[pl.ds(first_j(), n)], u, sem)
    copy.start()
    copy.wait()
    acc = mm(r[0], u[0])
    for q in range(1, n):
        acc = acc + mm(r[q], u[q])
    total[...] = acc
    half = keep.shape[0]
    core = core_of()
    keep[...] = total[pl.ds(pl.multiple_of(core * half, half), half), :]
    send[...] = total[pl.ds(pl.multiple_of((1 - core) * half, half), half), :]


def ladder_sum(r, factors, halfway):
    n, width, _ = r.shape
    rows = r[...].reshape(n * width, width)
    for p, b in enumerate(factors):
        h = mm_nt(b, rows).astype(BF16)
        for q in range(n):
            halfway[q * width : (q + 1) * width, p * width : (p + 1) * width] = h[:, q * width : (q + 1) * width]
    wide = factors[0] if len(factors) == 1 else jnp.concatenate(factors, 1)
    return mm_nt(wide, halfway[...])


def ladder_first(r, b, out, halfway):
    out[...] = ladder_sum(r, [b[...]], halfway)


def ladder_more(acc, r, b, out, halfway):
    out[...] = acc[...] + ladder_sum(r, [b[...]], halfway)


def pack(keep, got, piece, out):
    rows, width = piece.shape
    half, rank = keep.shape
    out[:rows] = piece[...]
    total = (keep[...] + got[...]).astype(BF16)
    folds = width // rank
    deep = half // folds
    for k in range(folds):
        out[rows:, k * rank : (k + 1) * rank] = total[k * deep : (k + 1) * deep]


def repack(rows, mine, theirs, out):
    out[:rows] = mine[:rows]
    out[rows : 2 * rows] = theirs[:rows]
    out[2 * rows :] = (mine[rows:].astype(F32) + theirs[rows:].astype(F32)).astype(BF16)


def place(pos, rows, mine, theirs, whole, latent):
    x, core = pos()
    for which, held in ((core, mine), (1 - core, theirs)):
        for k, half in enumerate((x, 1 - x)):
            at = pl.multiple_of((half * 2 + which) * rows, rows)
            whole[pl.ds(at, rows), :] = held[k * rows : (k + 1) * rows]
        half, rank = latent.shape[0] // 2, latent.shape[1]
        folds = whole.shape[1] // rank
        deep = half // folds
        for k in range(folds):
            at = pl.multiple_of(which * half + k * deep, deep)
            latent[pl.ds(at, deep), :] = held[2 * rows :, k * rank : (k + 1) * rank]


def ladder_packed(pos, rows, acc, r, mine, theirs, out, latent, whole, halfway):
    place(pos, rows, mine, theirs, whole, latent)
    out[...] = acc[...] + ladder_sum(r, [whole[...]], halfway)


def ladder_last(acc, r, b, latent, u, out, halfway, held, sems):
    n, width, _ = r.shape
    rows = r[...].reshape(n * width, width)
    h = mm_nt(b[...], rows).astype(BF16)
    for q in range(n):
        halfway[q * width : (q + 1) * width] = h[:, q * width : (q + 1) * width]
    copies = []
    for q in range(n):
        term = mm_nt(b[...], halfway[q * width : (q + 1) * width])
        cycle = mm_nt(latent[...], u[q]).astype(BF16)
        total = acc[:, q * width : (q + 1) * width] + term
        held[q] = (total + cycle.astype(F32)).astype(BF16)
        copies.append(pltpu.make_async_copy(held.at[q], out.at[q], sems.at[q]))
        copies[-1].start()
    for copy in copies:
        copy.wait()


def sigma_block(n_i, n_j, doubles, aux_factors, cycle_factors):
    rows_i, cols_j, width, _ = doubles.shape
    pairs = rows_i * cols_j
    rank = cycle_factors.shape[-1]
    r = doubles.reshape(pairs, width, width)
    own = aux_factors[0]
    quarter = width // 4
    flops = 2 * pairs * width * width * width

    def spot():
        j = lax.axis_index("ja")
        return lax.rem(lax.div(j, 2), 2), lax.rem(j, 2)

    def quarter_of():
        x, core = spot()
        return x * 2 + core

    core_swap = [(j, j ^ 1) for j in range(n_j)]
    chip_swap = [(j, j ^ 2) for j in range(n_j)]

    def ring(up, down):
        return [
            (i * n_j + j, (i + (down if j % 2 else up)) % n_i * n_j + j) for i in range(n_i) for j in range(n_j)
        ]

    piece = call(
        functools.partial(take_rows, quarter, quarter_of),
        pltpu.VMEM((quarter, width), BF16),
        [HBM],
        [pltpu.SemaphoreType.DMA],
        name="take",
    )(own)
    with jax.named_scope("far"):
        piece = lax.ppermute(piece, "ia", [(i, (i + n_i // 2) % n_i) for i in range(n_i)])
    near = []
    for step in range(1, n_i // 2):
        with jax.named_scope(f"near{step}"):
            near.append(lax.ppermute(own, ("ia", "ja"), ring(step, n_i - step)))

    keep, send, u = call(
        functools.partial(latent_part, lambda: spot()[1], lambda: lax.axis_index("ja") * cols_j),
        (pltpu.VMEM((width // 2, rank), F32), pltpu.VMEM((width // 2, rank), F32), pltpu.VMEM((cols_j, width, rank), BF16)),
        [VMEM, HBM],
        [pltpu.VMEM((width, rank), F32), pltpu.SemaphoreType.DMA],
        flops=2 * pairs * width * width * rank,
        moved=2 * pairs * width * width,
        name="latent_part",
    )(r, cycle_factors)
    with jax.named_scope("latent_cores"):
        got = lax.ppermute(send, "ja", core_swap)

    wide = pltpu.VMEM((width, pairs * width), F32)
    halfway = pltpu.VMEM((pairs * width, width), BF16)
    acc = call(ladder_first, wide, [VMEM] * 2, [halfway], flops=2 * flops, moved=pairs * width * width * 2, name="own")(r, own)

    fold = width // 2 * rank // width
    packed = call(pack, pltpu.VMEM((quarter + fold, width), BF16), [VMEM] * 3, name="pack")(keep, got, piece)
    with jax.named_scope("chips"):
        other = lax.ppermute(packed, "ja", chip_swap)
    packed = call(
        functools.partial(repack, quarter), pltpu.VMEM((2 * quarter + fold, width), BF16), [VMEM] * 2, name="repack"
    )(packed, other)
    apart = 4
    while apart < n_j:
        more = lax.ppermute(packed[2 * quarter :], "ja", [(j, j ^ apart) for j in range(n_j)])
        more = (packed[2 * quarter :].astype(F32) + more.astype(F32)).astype(BF16)
        packed = jnp.concatenate([packed[: 2 * quarter], more], 0)
        apart *= 2
    with jax.named_scope("cores"):
        other = lax.ppermute(packed, "ja", core_swap)
    swapped = []
    for step, factor in enumerate(near):
        with jax.named_scope(f"swap{step}"):
            swapped.append(lax.ppermute(factor, "ja", core_swap))

    acc, latent = call(
        functools.partial(ladder_packed, spot, quarter),
        (wide, pltpu.VMEM((width, rank), BF16)),
        [VMEM] * 4,
        [pltpu.VMEM((width, width), BF16), halfway],
        {0: 0},
        flops=2 * flops,
        moved=pairs * width * width * 2,
        name="far_term",
    )(acc, r, packed, other)
    for factor in near + swapped[:-1]:
        acc = call(
            ladder_more, wide, [VMEM] * 3, [halfway], {0: 0}, flops=2 * flops, moved=pairs * width * width * 2, name="term"
        )(acc, r, factor)
    out = call(
        ladder_last,
        jax.ShapeDtypeStruct((pairs, width, width), BF16),
        [VMEM] * 5,
        [halfway, pltpu.VMEM((pairs, width, width), BF16), pltpu.SemaphoreType.DMA((pairs,))],
        flops=2 * flops,
        moved=pairs * width * width * 2,
        name="last",
    )(acc, r, swapped[-1], latent, u)
    return out.reshape(doubles.shape)


def solution(mesh):
    n_i, n_j = mesh.shape["ia"], mesh.shape["ja"]
    in_specs = (P(("grp", "ia"), "ja", None, None), P("ia", None, None), P())
    out_specs = P(("grp", "ia"), "ja", None, None)
    block = functools.partial(sigma_block, n_i, n_j)
    return jax.shard_map(block, mesh=mesh, in_specs=in_specs, out_specs=out_specs, check_vma=False)
```

```python
import functools

import jax
import jax.numpy as jnp
from jax import lax
from jax.experimental import pallas as pl
from jax.experimental.pallas import tpu as pltpu
from jax.sharding import PartitionSpec as P

F32 = jnp.float32
BF16 = jnp.bfloat16
NT = (((1,), (1,)), ((), ()))
VMEM = pl.BlockSpec(memory_space=pltpu.VMEM)
HBM = pl.BlockSpec(memory_space=pltpu.HBM)


def call(kernel, outs, specs, scratch=(), aliases=None, flops=0, moved=0):
    return pl.pallas_call(
        kernel,
        out_shape=outs,
        in_specs=specs,
        out_specs=jax.tree.map(lambda o: VMEM if isinstance(o, pl.MemoryRef) else HBM, outs),
        scratch_shapes=scratch,
        input_output_aliases=aliases or {},
        cost_estimate=pl.CostEstimate(flops=flops, bytes_accessed=moved, transcendentals=0),
        compiler_params=pltpu.CompilerParams(vmem_limit_bytes=24 << 20),
    )


def in_hbm(x):
    return pltpu.with_memory_space_constraint(x, pltpu.HBM)


def mm(a, b):
    return jnp.dot(a, b, preferred_element_type=F32)


def mm_nt(a, b):
    return lax.dot_general(a, b, NT, preferred_element_type=F32)


def take_rows(rows, index_of, src, out, sem):
    start = pl.multiple_of(index_of() * rows, rows)
    copy = pltpu.make_async_copy(src.at[pl.ds(start, rows), :], out, sem)
    copy.start()
    copy.wait()


def latent_part(core_of, first_j, r_src, own_src, u_src, keep, send, r, own, u, total, sems):
    n = r.shape[0]
    copies = [pltpu.make_async_copy(u_src.at[pl.ds(first_j(), n)], u, sems.at[n])]
    copies += [pltpu.make_async_copy(r_src.at[q], r.at[q], sems.at[q]) for q in range(n)]
    copies += [pltpu.make_async_copy(own_src, own, sems.at[n + 1])]
    for copy in copies:
        copy.start()
    copies[0].wait()
    for q in range(n):
        copies[1 + q].wait()
        part = mm(r[q], u[q])
        total[...] = part if q == 0 else total[...] + part
    half = keep.shape[0]
    core = core_of()
    keep[...] = total[pl.ds(pl.multiple_of(core * half, half), half), :]
    send[...] = total[pl.ds(pl.multiple_of((1 - core) * half, half), half), :]
    copies[-1].wait()


def ladder_sum(r, factors, halfway):
    n, width, _ = r.shape
    rows = r[...].reshape(n * width, width)
    for p, b in enumerate(factors):
        h = mm_nt(b, rows).astype(BF16)
        for q in range(n):
            halfway[q * width : (q + 1) * width, p * width : (p + 1) * width] = h[:, q * width : (q + 1) * width]
    wide = factors[0] if len(factors) == 1 else jnp.concatenate(factors, 1)
    return mm_nt(wide, halfway[...])


def ladder_first(r, b, out, halfway):
    out[...] = ladder_sum(r, [b[...]], halfway)


def ladder_more(acc, r, b, out, halfway):
    out[...] = acc[...] + ladder_sum(r, [b[...]], halfway)


def pack(keep, got, piece, out):
    rows, width = piece.shape
    half, rank = keep.shape
    out[:rows] = piece[...]
    total = (keep[...] + got[...]).astype(BF16)
    folds = width // rank
    deep = half // folds
    for k in range(folds):
        out[rows:, k * rank : (k + 1) * rank] = total[k * deep : (k + 1) * deep]


def repack(rows, mine, theirs, out):
    out[:rows] = mine[:rows]
    out[rows : 2 * rows] = theirs[:rows]
    out[2 * rows :] = (mine[rows:].astype(F32) + theirs[rows:].astype(F32)).astype(BF16)


def place(pos, rows, mine, theirs, whole, latent):
    x, core = pos()
    for which, held in ((core, mine), (1 - core, theirs)):
        for k, half in enumerate((x, 1 - x)):
            at = pl.multiple_of((half * 2 + which) * rows, rows)
            whole[pl.ds(at, rows), :] = held[k * rows : (k + 1) * rows]
        half, rank = latent.shape[0] // 2, latent.shape[1]
        folds = whole.shape[1] // rank
        deep = half // folds
        for k in range(folds):
            at = pl.multiple_of(which * half + k * deep, deep)
            latent[pl.ds(at, deep), :] = held[2 * rows :, k * rank : (k + 1) * rank]


def ladder_last(pos, rows, acc, r, mine, theirs, u, out, whole, latent, halfway, held, sems):
    n, width, _ = r.shape
    place(pos, rows, mine, theirs, whole, latent)
    b = whole[...]
    h = mm_nt(b, r[...].reshape(n * width, width)).astype(BF16)
    for q in range(n):
        halfway[q * width : (q + 1) * width] = h[:, q * width : (q + 1) * width]
    copies = []
    for q in range(n):
        term = mm_nt(b, halfway[q * width : (q + 1) * width])
        cycle = mm_nt(latent[...], u[q]).astype(BF16)
        total = acc[:, q * width : (q + 1) * width] + term
        held[q] = (total + cycle.astype(F32)).astype(BF16)
        copies.append(pltpu.make_async_copy(held.at[q], out.at[q], sems.at[q]))
        copies[-1].start()
    for copy in copies:
        copy.wait()


def sigma_block(n_i, n_j, doubles, aux_factors, cycle_factors):
    rows_i, cols_j, width, _ = doubles.shape
    pairs = rows_i * cols_j
    rank = cycle_factors.shape[-1]
    r = doubles.reshape(pairs, width, width)
    own = aux_factors.reshape(width, width)
    quarter = width // 4
    flops = 2 * pairs * width * width * width

    def spot():
        j = lax.axis_index("ja")
        return lax.rem(lax.div(j, 2), 2), lax.rem(j, 2)

    def quarter_of():
        x, core = spot()
        return x * 2 + core

    core_swap = [(j, j ^ 1) for j in range(n_j)]
    chip_swap = [(j, j ^ 2) for j in range(n_j)]

    def ring(up, down):
        return [
            (i * n_j + j, (i + (down if j % 2 else up)) % n_i * n_j + j) for i in range(n_i) for j in range(n_j)
        ]

    piece = call(
        functools.partial(take_rows, quarter, quarter_of),
        pltpu.VMEM((quarter, width), BF16),
        [HBM],
        [pltpu.SemaphoreType.DMA],
    )(in_hbm(own))
    piece = lax.ppermute(piece, "ia", [(i, (i + n_i // 2) % n_i) for i in range(n_i)])
    near = []
    for step in range(1, n_i // 2):
        near.append(lax.ppermute(own, ("ia", "ja"), ring(step, n_i - step)))

    keep, send, r, own, u = call(
        functools.partial(latent_part, lambda: spot()[1], lambda: lax.axis_index("ja") * cols_j),
        (
            pltpu.VMEM((width // 2, rank), F32),
            pltpu.VMEM((width // 2, rank), F32),
            pltpu.VMEM((pairs, width, width), BF16),
            pltpu.VMEM((width, width), BF16),
            pltpu.VMEM((cols_j, width, rank), BF16),
        ),
        [HBM] * 3,
        [pltpu.VMEM((width, rank), F32), pltpu.SemaphoreType.DMA((pairs + 2,))],
        flops=2 * pairs * width * width * rank,
        moved=2 * pairs * width * width,
    )(in_hbm(r), in_hbm(own), in_hbm(cycle_factors))
    got = lax.ppermute(send, "ja", core_swap)

    wide = pltpu.VMEM((width, pairs * width), F32)
    halfway = pltpu.VMEM((pairs * width, width), BF16)
    acc = call(ladder_first, wide, [VMEM] * 2, [halfway], flops=2 * flops, moved=pairs * width * width * 2)(r, own)

    fold = width // 2 * rank // width
    packed = call(pack, pltpu.VMEM((quarter + fold, width), BF16), [VMEM] * 3)(keep, got, piece)
    other = lax.ppermute(packed, "ja", chip_swap)
    packed = call(
        functools.partial(repack, quarter), pltpu.VMEM((2 * quarter + fold, width), BF16), [VMEM] * 2
    )(packed, other)
    apart = 4
    while apart < n_j:
        more = lax.ppermute(packed[2 * quarter :], "ja", [(j, j ^ apart) for j in range(n_j)])
        more = (packed[2 * quarter :].astype(F32) + more.astype(F32)).astype(BF16)
        packed = jnp.concatenate([packed[: 2 * quarter], more], 0)
        apart *= 2
    other = lax.ppermute(packed, "ja", core_swap)
    swapped = []
    for factor in near:
        swapped.append(lax.ppermute(factor, "ja", core_swap))

    for factors in (near, swapped):
        for factor in factors:
            acc = call(
                ladder_more, wide, [VMEM] * 3, [halfway], {0: 0}, flops=2 * flops, moved=pairs * width * width * 2
            )(acc, r, factor)
    out = call(
        functools.partial(ladder_last, spot, quarter),
        jax.ShapeDtypeStruct((pairs, width, width), BF16),
        [VMEM] * 5,
        [
            pltpu.VMEM((width, width), BF16),
            pltpu.VMEM((width, rank), BF16),
            halfway,
            pltpu.VMEM((pairs, width, width), BF16),
            pltpu.SemaphoreType.DMA((pairs,)),
        ],
        flops=2 * flops,
        moved=pairs * width * width * 2,
    )(acc, r, packed, other, u)
    return out.reshape(doubles.shape)


def solution(mesh):
    n_i, n_j = mesh.shape["ia"], mesh.shape["ja"]
    in_specs = (P(("grp", "ia"), "ja", None, None), P("ia", None, None), P())
    out_specs = P(("grp", "ia"), "ja", None, None)

    def block(*args):
        return sigma_block(n_i, n_j, *args)

    return jax.shard_map(block, mesh=mesh, in_specs=in_specs, out_specs=out_specs, check_vma=False)
```

```python
import functools

import jax
import jax.numpy as jnp
from jax import lax
from jax.experimental import pallas as pl
from jax.experimental.pallas import tpu as pltpu
from jax.sharding import PartitionSpec as P

F32 = jnp.float32
BF16 = jnp.bfloat16
NT = (((1,), (1,)), ((), ()))
VMEM = pl.BlockSpec(memory_space=pltpu.VMEM)
HBM = pl.BlockSpec(memory_space=pltpu.HBM)


def call(kernel, outs, specs, scratch=(), aliases=None, flops=0, moved=0):
    return pl.pallas_call(
        kernel,
        out_shape=outs,
        in_specs=specs,
        out_specs=jax.tree.map(lambda o: VMEM if isinstance(o, pl.MemoryRef) else HBM, outs),
        scratch_shapes=scratch,
        input_output_aliases=aliases or {},
        cost_estimate=pl.CostEstimate(flops=flops, bytes_accessed=moved, transcendentals=0),
        compiler_params=pltpu.CompilerParams(vmem_limit_bytes=24 << 20),
    )


def in_hbm(x):
    return pltpu.with_memory_space_constraint(x, pltpu.HBM)


def mm(a, b):
    return jnp.dot(a, b, preferred_element_type=F32)


def mm_nt(a, b):
    return lax.dot_general(a, b, NT, preferred_element_type=F32)


def take_rows(where, src, *outs_and_sems):
    outs, sems = outs_and_sems[:2], outs_and_sems[2]
    copies = []
    for k, out in enumerate(outs):
        rows = out.shape[0]
        start = pl.multiple_of(where()[k] * rows, rows)
        copies.append(pltpu.make_async_copy(src.at[pl.ds(start, rows), :], out, sems.at[k]))
        copies[-1].start()
    for copy in copies:
        copy.wait()


def latent_part(first_j, r, u, out):
    j = first_j()
    acc = mm(r[0], u[j])
    for q in range(1, r.shape[0]):
        acc = acc + mm(r[q], u[j + q])
    out[...] = acc


def ladder_sum(r, factors, halfway):
    n, width, _ = r.shape
    rows = r[...].reshape(n * width, width)
    for p, b in enumerate(factors):
        h = mm_nt(b, rows).astype(BF16)
        for q in range(n):
            halfway[q * width : (q + 1) * width, p * width : (p + 1) * width] = h[:, q * width : (q + 1) * width]
    wide = factors[0] if len(factors) == 1 else jnp.concatenate(factors, 1)
    return mm_nt(wide, halfway[...])


def ladder_first(r, b, out, halfway):
    out[...] = ladder_sum(r, [b[...]], halfway)


def join(core, mine, theirs, whole):
    rows = mine.shape[0]
    whole[pl.ds(pl.multiple_of(core * rows, rows), rows), :] = mine[...]
    whole[pl.ds(pl.multiple_of((1 - core) * rows, rows), rows), :] = theirs[...]


def ladder_near(spot, acc, r, mine, theirs, out, whole, halfway):
    join(spot()[1], mine, theirs, whole)
    out[...] = acc[...] + ladder_sum(r, [whole[...]], halfway)


def pack(part, got, piece, out):
    rows, width = piece.shape
    rank = part.shape[1]
    out[:rows] = piece[...]
    total = (part[...] + got[...]).astype(BF16)
    deep = out.shape[0] - rows
    for k in range(width // rank):
        out[rows:, k * rank : (k + 1) * rank] = total[k * deep : (k + 1) * deep]


def repack(rows, mine, theirs, out):
    out[:rows] = mine[:rows]
    out[rows : 2 * rows] = theirs[:rows]
    out[2 * rows :] = (mine[rows:].astype(F32) + theirs[rows:].astype(F32)).astype(BF16)


def ladder_far(spot, first_j, rows, acc, r, mine, theirs, u, out, whole, latent, halfway):
    n, width, _ = r.shape
    parity, core = spot()
    for which, held in ((core, mine), (1 - core, theirs)):
        for k, half in enumerate((parity, 1 - parity)):
            at = pl.multiple_of((half * 2 + which) * rows, rows)
            whole[pl.ds(at, rows), :] = held[k * rows : (k + 1) * rows]
    folded = jnp.where(core == 0, mine[2 * rows :], theirs[2 * rows :])
    deep, rank = folded.shape[0], latent.shape[1]
    for k in range(width // rank):
        latent[k * deep : (k + 1) * deep] = folded[:, k * rank : (k + 1) * rank]
    out[...] = acc[...] + ladder_sum(r, [whole[...]], halfway)
    j = first_j()
    for q in range(n):
        cycle = mm_nt(latent[...], u[j + q]).astype(BF16)
        out[:, q * width : (q + 1) * width] += cycle.astype(F32)


def ladder_last(spot, acc, r, mine, theirs, out, whole, halfway, held, sems):
    n, width, _ = r.shape
    join(spot()[1], mine, theirs, whole)
    b = whole[...]
    h = mm_nt(b, r[...].reshape(n * width, width)).astype(BF16)
    for q in range(n):
        halfway[q * width : (q + 1) * width] = h[:, q * width : (q + 1) * width]
    copies = []
    for q in range(n):
        term = mm_nt(b, halfway[q * width : (q + 1) * width])
        held[q] = (acc[:, q * width : (q + 1) * width] + term).astype(BF16)
        copies.append(pltpu.make_async_copy(held.at[q], out.at[q], sems.at[q]))
        copies[-1].start()
    for copy in copies:
        copy.wait()


def sigma_block(n_i, n_j, doubles, aux_factors, cycle_factors):
    rows_i, cols_j, width, _ = doubles.shape
    pairs = rows_i * cols_j
    rank = cycle_factors.shape[-1]
    r = doubles.reshape(pairs, width, width)
    own = aux_factors.reshape(width, width)
    quarter, half = width // 4, width // 2
    fold = rank
    assert width % rank == 0 and fold * (width // rank) == width
    flops = 2 * pairs * width * width * width
    moved = 2 * pairs * width * width

    def spot():
        j = lax.axis_index("ja")
        return lax.rem(lax.div(j, 2) + lax.axis_index("grp"), 2), lax.rem(j, 2)

    def first_j():
        return lax.axis_index("ja") * cols_j

    def where():
        parity, core = spot()
        return parity * 2 + core, core

    def across(i, k):
        return i ^ k if n_i & (n_i - 1) == 0 else (i + k) % n_i

    core_swap = [(j, j ^ 1) for j in range(n_j)]
    chip_swap = [
        (g * n_j + j, (g ^ 1) * n_j + j if j % 2 else g * n_j + (j ^ 2)) for g in range(2) for j in range(n_j)
    ]
    far_away = n_i // 2

    piece, rows = call(
        functools.partial(take_rows, where),
        (pltpu.VMEM((quarter, width), BF16), pltpu.VMEM((half, width), BF16)),
        [HBM],
        [pltpu.SemaphoreType.DMA((2,))],
        flops=16 * flops,
        moved=8 * moved,
    )(in_hbm(own))
    piece = lax.ppermute(piece, "ia", [(i, across(i, far_away)) for i in range(n_i)])
    near = {}
    for k in range(1, n_i):
        if k != far_away:
            near[k] = lax.ppermute(rows, "ia", [(i, across(i, k)) for i in range(n_i)])

    part = call(
        functools.partial(latent_part, first_j),
        pltpu.VMEM((width, rank), F32),
        [VMEM] * 2,
        flops=flops * rank // width,
        moved=moved,
    )(r, cycle_factors)
    got = lax.ppermute(part, "ja", core_swap)

    wide = pltpu.VMEM((width, pairs * width), F32)
    whole = pltpu.VMEM((width, width), BF16)
    halfway = pltpu.VMEM((pairs * width, width), BF16)
    acc = call(ladder_first, wide, [VMEM] * 2, [halfway], flops=2 * flops, moved=moved)(r, own)

    packed = call(pack, pltpu.VMEM((quarter + fold, width), BF16), [VMEM] * 3)(part, got, piece)
    other = lax.ppermute(packed, ("grp", "ja"), chip_swap)
    packed = call(
        functools.partial(repack, quarter), pltpu.VMEM((2 * quarter + fold, width), BF16), [VMEM] * 2
    )(packed, other)
    apart = 4
    while apart < n_j:
        more = lax.ppermute(packed[2 * quarter :], "ja", [(j, j ^ apart) for j in range(n_j)])
        more = (packed[2 * quarter :].astype(F32) + more.astype(F32)).astype(BF16)
        packed = jnp.concatenate([packed[: 2 * quarter], more], 0)
        apart *= 2
    other = lax.ppermute(packed, "ja", core_swap)

    swapped = {}
    for k, mine in near.items():
        swapped[k] = lax.ppermute(mine, "ja", core_swap)
    *before, last = near
    for k in before:
        acc = call(
            functools.partial(ladder_near, spot),
            wide,
            [VMEM] * 4,
            [whole, halfway],
            {0: 0},
            flops=2 * flops,
            moved=moved,
        )(acc, r, near[k], swapped[k])
    acc = call(
        functools.partial(ladder_far, spot, first_j, quarter),
        wide,
        [VMEM] * 5,
        [whole, pltpu.VMEM((width, rank), BF16), halfway],
        {0: 0},
        flops=2 * flops,
        moved=moved,
    )(acc, r, packed, other, cycle_factors)
    out = call(
        functools.partial(ladder_last, spot),
        jax.ShapeDtypeStruct((pairs, width, width), BF16),
        [VMEM] * 4,
        [whole, halfway, pltpu.VMEM((pairs, width, width), BF16), pltpu.SemaphoreType.DMA((pairs,))],
        flops=2 * flops,
        moved=moved,
    )(acc, r, near[last], swapped[last])
    return out.reshape(doubles.shape)


def solution(mesh):
    n_i, n_j = mesh.shape["ia"], mesh.shape["ja"]
    in_specs = (P(("grp", "ia"), "ja", None, None), P("ia", None, None), P())
    out_specs = P(("grp", "ia"), "ja", None, None)

    def block(*args):
        return sigma_block(n_i, n_j, *args)

    return jax.shard_map(block, mesh=mesh, in_specs=in_specs, out_specs=out_specs, check_vma=False)
```

```python
import functools

import jax
import jax.numpy as jnp
from jax import lax
from jax.experimental import pallas as pl
from jax.experimental.pallas import tpu as pltpu
from jax.sharding import PartitionSpec as P

F32 = jnp.float32
BF16 = jnp.bfloat16
NT = (((1,), (1,)), ((), ()))
VMEM = pl.BlockSpec(memory_space=pltpu.VMEM)
HBM = pl.BlockSpec(memory_space=pltpu.HBM)


def call(kernel, outs, specs, scratch=(), aliases=None, flops=0, moved=0):
    return pl.pallas_call(
        kernel,
        out_shape=outs,
        in_specs=specs,
        out_specs=jax.tree.map(lambda o: VMEM if isinstance(o, pl.MemoryRef) else HBM, outs),
        scratch_shapes=scratch,
        input_output_aliases=aliases or {},
        cost_estimate=pl.CostEstimate(flops=flops, bytes_accessed=moved, transcendentals=0),
        compiler_params=pltpu.CompilerParams(vmem_limit_bytes=24 << 20),
    )


def in_hbm(x):
    return pltpu.with_memory_space_constraint(x, pltpu.HBM)


def mm(a, b):
    return jnp.dot(a, b, preferred_element_type=F32)


def mm_nt(a, b):
    return lax.dot_general(a, b, NT, preferred_element_type=F32)


def take_far(index_of, src, out, sems):
    rows = out.shape[0] // 3
    start = index_of() * out.shape[0]
    copies = [
        pltpu.make_async_copy(
            src.at[pl.ds(pl.multiple_of(start + k * rows, rows), rows), :],
            out.at[pl.ds(k * rows, rows), :],
            sems.at[k],
        )
        for k in range(3)
    ]
    for copy in copies:
        copy.start()
    for copy in copies:
        copy.wait()


def take_near(index_of, src, out):
    rows = out.shape[0]
    out[...] = src[pl.ds(pl.multiple_of(index_of() * rows, rows), rows), :]


def latent_part(first_j, r, u, out):
    j = first_j()
    acc = mm(r[0], u[j])
    for q in range(1, r.shape[0]):
        acc = acc + mm(r[q], u[j + q])
    out[...] = acc


def ladder_sum(r, factors, halfway):
    n, width, _ = r.shape
    rows = r[...].reshape(n * width, width)
    for p, b in enumerate(factors):
        h = mm_nt(b, rows).astype(BF16)
        for q in range(n):
            halfway[q * width : (q + 1) * width, p * width : (p + 1) * width] = h[:, q * width : (q + 1) * width]
    wide = factors[0] if len(factors) == 1 else jnp.concatenate(factors, 1)
    return mm_nt(wide, halfway[...])


def ladder_first(r, b, out, halfway):
    out[...] = ladder_sum(r, [b[...]], halfway)


def join(core, mine, theirs, whole):
    rows = mine.shape[0]
    whole[pl.ds(pl.multiple_of(core * rows, rows), rows), :] = mine[...]
    whole[pl.ds(pl.multiple_of((1 - core) * rows, rows), rows), :] = theirs[...]


def ladder_near(spot, acc, r, mine, theirs, out, whole, halfway):
    join(spot()[1], mine, theirs, whole)
    out[...] = acc[...] + ladder_sum(r, [whole[...]], halfway)


def pack(part, got, piece, out):
    rows, width = piece.shape
    rank = part.shape[1]
    out[:rows] = piece[...]
    total = (part[...] + got[...]).astype(BF16)
    deep = out.shape[0] - rows
    for k in range(width // rank):
        out[rows:, k * rank : (k + 1) * rank] = total[k * deep : (k + 1) * deep]


def repack(rows, mine, theirs, out):
    out[:rows] = mine[:rows]
    out[rows : 2 * rows] = theirs[:rows]
    out[2 * rows :] = (mine[rows:].astype(F32) + theirs[rows:].astype(F32)).astype(BF16)


def first_products(r, pieces, halfway):
    n, width, _ = r.shape
    stack = jnp.concatenate([rows for rows, _, _ in pieces], 0)
    for g in range(0, n, 2):
        h = mm_nt(stack, r[g : g + 2].reshape(2 * width, width)).astype(BF16)
        top = 0
        for rows, p, start in pieces:
            size = rows.shape[0]
            for k in range(2):
                at = pl.multiple_of((g + k) * width + start, size)
                halfway[pl.ds(at, size), p * width : (p + 1) * width] = h[top : top + size, k * width : (k + 1) * width]
            top += size


def held_rows(spot, rows, which, packed, near):
    parity, _ = spot()
    half = near.shape[0]
    return [
        (packed[:rows], 0, (parity * 2 + which) * rows),
        (packed[rows : 2 * rows], 0, ((1 - parity) * 2 + which) * rows),
        (near[...], 1, which * half),
    ]


def ladder_ahead(spot, rows, r, packed, near, halfway):
    first_products(r, held_rows(spot, rows, spot()[1], packed, near), halfway)


def ladder_last(
    spot, first_j, rows, acc, r, packed, other, near, swapped, u, ahead, out, halfway, wide, latent, held, sems
):
    n, width, _ = r.shape
    core = spot()[1]
    theirs = held_rows(spot, rows, 1 - core, other, swapped)
    first_products(r, theirs, halfway)
    for piece, p, start in held_rows(spot, rows, core, packed, near) + theirs:
        size = piece.shape[0]
        wide[pl.ds(pl.multiple_of(start, size), size), p * width : (p + 1) * width] = piece
    folded = jnp.where(core == 0, packed[2 * rows :], other[2 * rows :])
    deep, rank = folded.shape[0], latent.shape[1]
    for k in range(width // rank):
        latent[k * deep : (k + 1) * deep] = folded[:, k * rank : (k + 1) * rank]
    j = first_j()
    copies = []
    for g in range(0, n, 2):
        span = slice(g * width, (g + 2) * width)
        term = mm_nt(wide[...], halfway[span])
        cycle = mm_nt(latent[...], u[pl.ds(j + g, 2)].reshape(2 * width, rank)).astype(BF16)
        total = (acc[:, span] + term + cycle.astype(F32)).astype(BF16)
        for k in range(2):
            held[g + k] = total[:, k * width : (k + 1) * width]
            copies.append(pltpu.make_async_copy(held.at[g + k], out.at[g + k], sems.at[g + k]))
            copies[-1].start()
    for copy in copies:
        copy.wait()


def sigma_block(n_i, n_j, doubles, aux_factors, cycle_factors):
    rows_i, cols_j, width, _ = doubles.shape
    pairs = rows_i * cols_j
    rank = cycle_factors.shape[-1]
    r = doubles.reshape(pairs, width, width)
    own = aux_factors.reshape(width, width)
    quarter, half = width // 4, width // 2
    fold = rank
    assert width % rank == 0 and fold * (width // rank) == width
    flops = 2 * pairs * width * width * width
    moved = 2 * pairs * width * width

    def spot():
        j = lax.axis_index("ja")
        return lax.rem(lax.div(j, 2) + lax.axis_index("grp"), 2), lax.rem(j, 2)

    def first_j():
        return lax.axis_index("ja") * cols_j

    def quarter_of():
        parity, core = spot()
        return parity * 2 + core

    def across(i, k):
        return i ^ k if n_i & (n_i - 1) == 0 else (i + k) % n_i

    core_swap = [(j, j ^ 1) for j in range(n_j)]
    chip_swap = [
        (g * n_j + j, (g ^ 1) * n_j + j if j % 2 else g * n_j + (j ^ 2)) for g in range(2) for j in range(n_j)
    ]
    far_away = n_i // 2

    piece = call(
        functools.partial(take_far, quarter_of),
        pltpu.VMEM((quarter, width), BF16),
        [HBM],
        [pltpu.SemaphoreType.DMA((3,))],
        flops=2 * flops,
        moved=moved * 2 // 2,
    )(in_hbm(own))
    piece = lax.ppermute(piece, "ia", [(i, across(i, far_away)) for i in range(n_i)])
    rows = call(
        functools.partial(take_near, lambda: spot()[1]),
        pltpu.VMEM((half, width), BF16),
        [VMEM],
        flops=16 * flops,
        moved=8 * moved,
    )(own)
    near = {}
    for k in range(1, n_i):
        if k != far_away:
            near[k] = lax.ppermute(rows, "ia", [(i, across(i, k)) for i in range(n_i)])

    part = call(
        functools.partial(latent_part, first_j),
        pltpu.VMEM((width, rank), F32),
        [VMEM] * 2,
        flops=flops * rank // width,
        moved=moved,
    )(r, cycle_factors)
    got = lax.ppermute(part, "ja", core_swap)

    wide = pltpu.VMEM((width, pairs * width), F32)
    whole = pltpu.VMEM((width, width), BF16)
    halfway = pltpu.VMEM((pairs * width, width), BF16)
    acc = call(ladder_first, wide, [VMEM] * 2, [halfway], flops=2 * flops, moved=moved)(r, own)

    packed = call(pack, pltpu.VMEM((quarter + fold, width), BF16), [VMEM] * 3)(part, got, piece)
    other = lax.ppermute(packed, ("grp", "ja"), chip_swap)
    packed = call(
        functools.partial(repack, quarter), pltpu.VMEM((2 * quarter + fold, width), BF16), [VMEM] * 2
    )(packed, other)
    apart = 4
    while apart < n_j:
        more = lax.ppermute(packed[2 * quarter :], "ja", [(j, j ^ apart) for j in range(n_j)])
        more = (packed[2 * quarter :].astype(F32) + more.astype(F32)).astype(BF16)
        packed = jnp.concatenate([packed[: 2 * quarter], more], 0)
        apart *= 2
    other = lax.ppermute(packed, "ja", core_swap)

    swapped = {}
    for k, mine in near.items():
        swapped[k] = lax.ppermute(mine, "ja", core_swap)
    *before, last = near
    for k in before:
        acc = call(
            functools.partial(ladder_near, spot),
            wide,
            [VMEM] * 4,
            [whole, halfway],
            {0: 0},
            flops=2 * flops,
            moved=moved,
        )(acc, r, near[k], swapped[k])
    ahead = call(
        functools.partial(ladder_ahead, spot, quarter),
        pltpu.VMEM((pairs * width, 2 * width), BF16),
        [VMEM] * 3,
        flops=flops,
        moved=moved,
    )(r, packed, near[last])
    out, _ = call(
        functools.partial(ladder_last, spot, first_j, quarter),
        (jax.ShapeDtypeStruct((pairs, width, width), BF16), pltpu.VMEM((pairs * width, 2 * width), BF16)),
        [VMEM] * 8,
        [
            pltpu.VMEM((width, 2 * width), BF16),
            pltpu.VMEM((width, rank), BF16),
            pltpu.VMEM((pairs, width, width), BF16),
            pltpu.SemaphoreType.DMA((pairs,)),
        ],
        {7: 1},
        flops=3 * flops,
        moved=2 * moved,
    )(acc, r, packed, other, near[last], swapped[last], cycle_factors, ahead)
    return out.reshape(doubles.shape)


def solution(mesh):
    n_i, n_j = mesh.shape["ia"], mesh.shape["ja"]
    in_specs = (P(("grp", "ia"), "ja", None, None), P("ia", None, None), P())
    out_specs = P(("grp", "ia"), "ja", None, None)

    def block(*args):
        return sigma_block(n_i, n_j, *args)

    return jax.shard_map(block, mesh=mesh, in_specs=in_specs, out_specs=out_specs, check_vma=False)
```

```python
import functools

import jax
import jax.numpy as jnp
from jax import lax
from jax.experimental import pallas as pl
from jax.experimental.pallas import tpu as pltpu
from jax.sharding import PartitionSpec as P

F32 = jnp.float32
BF16 = jnp.bfloat16
NT = (((1,), (1,)), ((), ()))
VMEM = pl.BlockSpec(memory_space=pltpu.VMEM)
HBM = pl.BlockSpec(memory_space=pltpu.HBM)


def call(kernel, outs, specs, scratch=(), aliases=None, flops=0, moved=0):
    return pl.pallas_call(
        kernel,
        out_shape=outs,
        in_specs=specs,
        out_specs=jax.tree.map(lambda o: VMEM if isinstance(o, pl.MemoryRef) else HBM, outs),
        scratch_shapes=scratch,
        input_output_aliases=aliases or {},
        cost_estimate=pl.CostEstimate(flops=flops, bytes_accessed=moved, transcendentals=0),
        compiler_params=pltpu.CompilerParams(vmem_limit_bytes=24 << 20),
    )


def in_hbm(x):
    return pltpu.with_memory_space_constraint(x, pltpu.HBM)


def mm(a, b):
    return jnp.dot(a, b, preferred_element_type=F32)


def mm_nt(a, b):
    return lax.dot_general(a, b, NT, preferred_element_type=F32)


def take_far(index_of, src, out, sems):
    count = sems.shape[0]
    rows = out.shape[0] // count
    copies = []
    for k in range(count):
        at = pl.multiple_of((index_of() * count + k) * rows, rows)
        copies.append(pltpu.make_async_copy(src.at[pl.ds(at, rows), :], out.at[pl.ds(k * rows, rows), :], sems.at[k]))
        copies[-1].start()
    for copy in copies:
        copy.wait()


def take_near(index_of, src, out):
    rows = out.shape[0]
    out[...] = src[pl.ds(pl.multiple_of(index_of() * rows, rows), rows), :]


def latent_part(first_j, r, u, out):
    j = first_j()
    acc = mm(r[0], u[j])
    for q in range(1, r.shape[0]):
        acc = acc + mm(r[q], u[j + q])
    out[...] = acc


def ladder_sum(r, factors, halfway):
    n, width, _ = r.shape
    rows = r[...].reshape(n * width, width)
    for p, b in enumerate(factors):
        h = mm_nt(b, rows).astype(BF16)
        for q in range(n):
            halfway[q * width : (q + 1) * width, p * width : (p + 1) * width] = h[:, q * width : (q + 1) * width]
    wide = factors[0] if len(factors) == 1 else jnp.concatenate(factors, 1)
    return mm_nt(wide, halfway[...])


def ladder_first(r, b, out, halfway):
    out[...] = ladder_sum(r, [b[...]], halfway)


def join(core, mine, theirs, whole):
    rows = mine.shape[0]
    whole[pl.ds(pl.multiple_of(core * rows, rows), rows), :] = mine[...]
    whole[pl.ds(pl.multiple_of((1 - core) * rows, rows), rows), :] = theirs[...]


def ladder_near(spot, acc, r, mine, theirs, out, whole, halfway):
    join(spot()[1], mine, theirs, whole)
    out[...] = acc[...] + ladder_sum(r, [whole[...]], halfway)


def pack(part, got, piece, out):
    rows, width = piece.shape
    rank = part.shape[1]
    out[:rows] = piece[...]
    total = (part[...] + got[...]).astype(BF16)
    deep = out.shape[0] - rows
    for k in range(width // rank):
        out[rows:, k * rank : (k + 1) * rank] = total[k * deep : (k + 1) * deep]


def repack(rows, mine, theirs, out):
    out[:rows] = mine[:rows]
    out[rows : 2 * rows] = theirs[:rows]
    out[2 * rows :] = (mine[rows:].astype(F32) + theirs[rows:].astype(F32)).astype(BF16)


def first_products(r, pieces, halfway):
    n, width, _ = r.shape
    stack = jnp.concatenate([rows for rows, _, _ in pieces], 0)
    for g in range(0, n, 2):
        h = mm_nt(stack, r[g : g + 2].reshape(2 * width, width)).astype(BF16)
        top = 0
        for rows, p, start in pieces:
            size = rows.shape[0]
            for k in range(2):
                at = pl.multiple_of((g + k) * width + start, size)
                halfway[pl.ds(at, size), p * width : (p + 1) * width] = h[top : top + size, k * width : (k + 1) * width]
            top += size


def held_rows(spot, rows, which, packed, near):
    parity, _ = spot()
    half = near.shape[0]
    return [
        (packed[:rows], 0, (parity * 2 + which) * rows),
        (packed[rows : 2 * rows], 0, ((1 - parity) * 2 + which) * rows),
        (near[...], 1, which * half),
    ]


def ladder_ahead(spot, rows, r, packed, near, halfway):
    first_products(r, held_rows(spot, rows, spot()[1], packed, near), halfway)


def ladder_last(
    spot, first_j, rows, acc, r, packed, other, near, swapped, u, ahead, out, halfway, wide, latent, held, sems
):
    n, width, _ = r.shape
    core = spot()[1]
    theirs = held_rows(spot, rows, 1 - core, other, swapped)
    first_products(r, theirs, halfway)
    for piece, p, start in held_rows(spot, rows, core, packed, near) + theirs:
        size = piece.shape[0]
        wide[pl.ds(pl.multiple_of(start, size), size), p * width : (p + 1) * width] = piece
    folded = jnp.where(core == 0, packed[2 * rows :], other[2 * rows :])
    deep, rank = folded.shape[0], latent.shape[1]
    for k in range(width // rank):
        latent[k * deep : (k + 1) * deep] = folded[:, k * rank : (k + 1) * rank]
    j = first_j()
    copies = []
    for g in range(0, n, 2):
        span = slice(g * width, (g + 2) * width)
        term = mm_nt(wide[...], halfway[span])
        cycle = mm_nt(latent[...], u[pl.ds(j + g, 2)].reshape(2 * width, rank)).astype(BF16)
        total = (acc[:, span] + term + cycle.astype(F32)).astype(BF16)
        for k in range(2):
            held[g + k] = total[:, k * width : (k + 1) * width]
            copies.append(pltpu.make_async_copy(held.at[g + k], out.at[g + k], sems.at[g + k]))
            copies[-1].start()
    for copy in copies:
        copy.wait()


def sigma_block(n_g, n_i, n_j, doubles, aux_factors, cycle_factors):
    rows_i, cols_j, width, _ = doubles.shape
    pairs = rows_i * cols_j
    rank = cycle_factors.shape[-1]
    r = doubles.reshape(pairs, width, width)
    own = aux_factors.reshape(width, width)
    quarter, half = width // 4, width // 2
    fold = rank
    assert width % rank == 0 and pairs % 2 == 0 and n_g % 2 == 0 and n_j % 4 == 0
    flops = 2 * pairs * width * width * width
    moved = 2 * pairs * width * width

    def spot():
        j = lax.axis_index("ja")
        return lax.rem(lax.div(j, 2) + lax.axis_index("grp"), 2), lax.rem(j, 2)

    def first_j():
        return lax.axis_index("ja") * cols_j

    def quarter_of():
        parity, core = spot()
        return parity * 2 + core

    def across(i, k):
        return i ^ k if n_i & (n_i - 1) == 0 else (i + k) % n_i

    core_swap = [(j, j ^ 1) for j in range(n_j)]
    chip_swap = [
        (g * n_j + j, (g ^ 1) * n_j + j if j % 2 else g * n_j + (j ^ 2)) for g in range(n_g) for j in range(n_j)
    ]
    far_away = n_i // 2

    piece = call(
        functools.partial(take_far, quarter_of),
        pltpu.VMEM((quarter, width), BF16),
        [HBM],
        [pltpu.SemaphoreType.DMA((3 if quarter % 48 == 0 else 1,))],
        flops=2 * flops,
        moved=moved * 2 // 2,
    )(in_hbm(own))
    piece = lax.ppermute(piece, "ia", [(i, across(i, far_away)) for i in range(n_i)])
    rows = call(
        functools.partial(take_near, lambda: spot()[1]),
        pltpu.VMEM((half, width), BF16),
        [VMEM],
        flops=16 * flops,
        moved=8 * moved,
    )(own)
    near = {}
    for k in range(1, n_i):
        if k != far_away:
            near[k] = lax.ppermute(rows, "ia", [(i, across(i, k)) for i in range(n_i)])

    part = call(
        functools.partial(latent_part, first_j),
        pltpu.VMEM((width, rank), F32),
        [VMEM] * 2,
        flops=flops * rank // width,
        moved=moved,
    )(r, cycle_factors)
    got = lax.ppermute(part, "ja", core_swap)

    wide = pltpu.VMEM((width, pairs * width), F32)
    whole = pltpu.VMEM((width, width), BF16)
    halfway = pltpu.VMEM((pairs * width, width), BF16)
    acc = call(ladder_first, wide, [VMEM] * 2, [halfway], flops=2 * flops, moved=moved)(r, own)

    packed = call(pack, pltpu.VMEM((quarter + fold, width), BF16), [VMEM] * 3)(part, got, piece)
    other = lax.ppermute(packed, ("grp", "ja"), chip_swap)
    packed = call(
        functools.partial(repack, quarter), pltpu.VMEM((2 * quarter + fold, width), BF16), [VMEM] * 2
    )(packed, other)
    apart = 4
    while apart < n_j:
        more = lax.ppermute(packed[2 * quarter :], "ja", [(j, j ^ apart) for j in range(n_j)])
        more = (packed[2 * quarter :].astype(F32) + more.astype(F32)).astype(BF16)
        packed = jnp.concatenate([packed[: 2 * quarter], more], 0)
        apart *= 2
    other = lax.ppermute(packed, "ja", core_swap)

    swapped = {}
    for k, mine in near.items():
        swapped[k] = lax.ppermute(mine, "ja", core_swap)
    *before, last = near
    for k in before:
        acc = call(
            functools.partial(ladder_near, spot),
            wide,
            [VMEM] * 4,
            [whole, halfway],
            {0: 0},
            flops=2 * flops,
            moved=moved,
        )(acc, r, near[k], swapped[k])
    ahead = call(
        functools.partial(ladder_ahead, spot, quarter),
        pltpu.VMEM((pairs * width, 2 * width), BF16),
        [VMEM] * 3,
        flops=flops,
        moved=moved,
    )(r, packed, near[last])
    out, _ = call(
        functools.partial(ladder_last, spot, first_j, quarter),
        (jax.ShapeDtypeStruct((pairs, width, width), BF16), pltpu.VMEM((pairs * width, 2 * width), BF16)),
        [VMEM] * 8,
        [
            pltpu.VMEM((width, 2 * width), BF16),
            pltpu.VMEM((width, rank), BF16),
            pltpu.VMEM((pairs, width, width), BF16),
            pltpu.SemaphoreType.DMA((pairs,)),
        ],
        {7: 1},
        flops=3 * flops,
        moved=2 * moved,
    )(acc, r, packed, other, near[last], swapped[last], cycle_factors, ahead)
    return out.reshape(doubles.shape)


def solution(mesh):
    n_g, n_i, n_j = (mesh.shape[axis] for axis in ("grp", "ia", "ja"))
    in_specs = (P(("grp", "ia"), "ja", None, None), P("ia", None, None), P())
    out_specs = P(("grp", "ia"), "ja", None, None)

    def block(*args):
        return sigma_block(n_g, n_i, n_j, *args)

    return jax.shard_map(block, mesh=mesh, in_specs=in_specs, out_specs=out_specs, check_vma=False)
```

```python
import functools

import jax
import jax.numpy as jnp
from jax import lax
from jax.experimental import pallas as pl
from jax.experimental.pallas import tpu as pltpu
from jax.sharding import PartitionSpec as P

F32 = jnp.float32
BF16 = jnp.bfloat16
NT = (((1,), (1,)), ((), ()))
VMEM = pl.BlockSpec(memory_space=pltpu.VMEM)
HBM = pl.BlockSpec(memory_space=pltpu.HBM)


def call(kernel, outs, specs, scratch=(), aliases=None, flops=0, moved=0):
    return pl.pallas_call(
        kernel,
        out_shape=outs,
        in_specs=specs,
        out_specs=jax.tree.map(lambda o: VMEM if isinstance(o, pl.MemoryRef) else HBM, outs),
        scratch_shapes=scratch,
        input_output_aliases=aliases or {},
        cost_estimate=pl.CostEstimate(flops=flops, bytes_accessed=moved, transcendentals=0),
        compiler_params=pltpu.CompilerParams(vmem_limit_bytes=24 << 20),
    )


def in_hbm(x):
    return pltpu.with_memory_space_constraint(x, pltpu.HBM)


def mm(a, b):
    return jnp.dot(a, b, preferred_element_type=F32)


def mm_nt(a, b):
    return lax.dot_general(a, b, NT, preferred_element_type=F32)


def take_far(index_of, src, out, sems):
    count = sems.shape[0]
    rows = out.shape[0] // count
    copies = []
    for k in range(count):
        at = pl.multiple_of((index_of() * count + k) * rows, rows)
        copies.append(pltpu.make_async_copy(src.at[pl.ds(at, rows), :], out.at[pl.ds(k * rows, rows), :], sems.at[k]))
        copies[-1].start()
    for copy in copies:
        copy.wait()


def take_near(index_of, src, out):
    rows = out.shape[0]
    out[...] = src[pl.ds(pl.multiple_of(index_of() * rows, rows), rows), :]


def latent_part(first_j, r, u, out):
    j = first_j()
    acc = mm(r[0], u[j])
    for q in range(1, r.shape[0]):
        acc = acc + mm(r[q], u[j + q])
    out[...] = acc


def ladder_sum(r, factors, halfway):
    n, width, _ = r.shape
    rows = r[...].reshape(n * width, width)
    for p, b in enumerate(factors):
        h = mm_nt(b, rows).astype(BF16)
        for q in range(n):
            halfway[q * width : (q + 1) * width, p * width : (p + 1) * width] = h[:, q * width : (q + 1) * width]
    wide = factors[0] if len(factors) == 1 else jnp.concatenate(factors, 1)
    return mm_nt(wide, halfway[...])


def ladder_first(r, b, out, halfway):
    out[...] = ladder_sum(r, [b[...]], halfway)


def join(core, mine, theirs, whole):
    rows = mine.shape[0]
    whole[pl.ds(pl.multiple_of(core * rows, rows), rows), :] = mine[...]
    whole[pl.ds(pl.multiple_of((1 - core) * rows, rows), rows), :] = theirs[...]


def ladder_near(spot, acc, r, mine, theirs, out, whole, halfway):
    join(spot()[1], mine, theirs, whole)
    out[...] = acc[...] + ladder_sum(r, [whole[...]], halfway)


def pack(part, got, piece, out):
    rows, width = piece.shape
    rank = part.shape[1]
    out[:rows] = piece[...]
    total = (part[...] + got[...]).astype(BF16)
    deep = out.shape[0] - rows
    for k in range(width // rank):
        out[rows:, k * rank : (k + 1) * rank] = total[k * deep : (k + 1) * deep]


def repack(rows, mine, theirs, out):
    out[:rows] = mine[:rows]
    out[rows : 2 * rows] = theirs[:rows]
    out[2 * rows :] = (mine[rows:].astype(F32) + theirs[rows:].astype(F32)).astype(BF16)


def first_products(r, pieces):
    n, width, _ = r.shape
    stack = jnp.concatenate([rows for rows, _, _ in pieces], 0)
    return mm_nt(stack, r[...].reshape(n * width, width)).astype(BF16)


def spread(products, pieces, halfway):
    width = halfway.shape[1] // 2
    top = 0
    for rows, p, start in pieces:
        size = rows.shape[0]
        for q in range(halfway.shape[0] // width):
            at = pl.multiple_of(q * width + start, size)
            halfway[pl.ds(at, size), p * width : (p + 1) * width] = products[
                top : top + size, q * width : (q + 1) * width
            ]
        top += size


def held_rows(spot, rows, which, packed, near):
    parity, _ = spot()
    half = near.shape[0]
    return [
        (packed[:rows], 0, (parity * 2 + which) * rows),
        (packed[rows : 2 * rows], 0, ((1 - parity) * 2 + which) * rows),
        (near[...], 1, which * half),
    ]


def ladder_ahead(spot, rows, r, packed, near, out):
    out[...] = first_products(r, held_rows(spot, rows, spot()[1], packed, near))


def ladder_last(
    spot, first_j, rows, acc, r, packed, other, near, swapped, u, ahead, out, halfway, wide, latent, held, sems
):
    n, width, _ = r.shape
    core = spot()[1]
    ours = held_rows(spot, rows, core, packed, near)
    theirs = held_rows(spot, rows, 1 - core, other, swapped)
    spread(ahead, ours, halfway)
    spread(first_products(r, theirs), theirs, halfway)
    for piece, p, start in ours + theirs:
        size = piece.shape[0]
        wide[pl.ds(pl.multiple_of(start, size), size), p * width : (p + 1) * width] = piece
    folded = jnp.where(core == 0, packed[2 * rows :], other[2 * rows :])
    deep, rank = folded.shape[0], latent.shape[1]
    for k in range(width // rank):
        latent[k * deep : (k + 1) * deep] = folded[:, k * rank : (k + 1) * rank]
    j = first_j()
    copies = []
    for g in range(0, n, 2):
        span = slice(g * width, (g + 2) * width)
        term = mm_nt(wide[...], halfway[span])
        cycle = mm_nt(latent[...], u[pl.ds(j + g, 2)].reshape(2 * width, rank)).astype(BF16)
        total = (acc[:, span] + term + cycle.astype(F32)).astype(BF16)
        for k in range(2):
            held[g + k] = total[:, k * width : (k + 1) * width]
            copies.append(pltpu.make_async_copy(held.at[g + k], out.at[g + k], sems.at[g + k]))
            copies[-1].start()
    for copy in copies:
        copy.wait()


def sigma_block(n_g, n_i, n_j, doubles, aux_factors, cycle_factors):
    rows_i, cols_j, width, _ = doubles.shape
    pairs = rows_i * cols_j
    rank = cycle_factors.shape[-1]
    r = doubles.reshape(pairs, width, width)
    own = aux_factors.reshape(width, width)
    quarter, half = width // 4, width // 2
    fold = rank
    assert width % rank == 0 and pairs % 2 == 0 and n_g % 2 == 0 and n_j % 4 == 0
    flops = 2 * pairs * width * width * width
    moved = 2 * pairs * width * width

    def spot():
        j = lax.axis_index("ja")
        return lax.rem(lax.div(j, 2) + lax.axis_index("grp"), 2), lax.rem(j, 2)

    def first_j():
        return lax.axis_index("ja") * cols_j

    def quarter_of():
        parity, core = spot()
        return parity * 2 + core

    def across(i, k):
        return i ^ k if n_i & (n_i - 1) == 0 else (i + k) % n_i

    core_swap = [(j, j ^ 1) for j in range(n_j)]
    chip_swap = [
        (g * n_j + j, (g ^ 1) * n_j + j if j % 2 else g * n_j + (j ^ 2)) for g in range(n_g) for j in range(n_j)
    ]
    far_away = n_i // 2

    piece = call(
        functools.partial(take_far, quarter_of),
        pltpu.VMEM((quarter, width), BF16),
        [HBM],
        [pltpu.SemaphoreType.DMA((3 if quarter % 48 == 0 else 1,))],
        flops=2 * flops,
        moved=moved * 2 // 2,
    )(in_hbm(own))
    piece = lax.ppermute(piece, "ia", [(i, across(i, far_away)) for i in range(n_i)])
    rows = call(
        functools.partial(take_near, lambda: spot()[1]),
        pltpu.VMEM((half, width), BF16),
        [VMEM],
        flops=16 * flops,
        moved=8 * moved,
    )(own)
    near = {}
    for k in range(1, n_i):
        if k != far_away:
            near[k] = lax.ppermute(rows, "ia", [(i, across(i, k)) for i in range(n_i)])

    part = call(
        functools.partial(latent_part, first_j),
        pltpu.VMEM((width, rank), F32),
        [VMEM] * 2,
        flops=flops * rank // width,
        moved=moved,
    )(r, cycle_factors)
    got = lax.ppermute(part, "ja", core_swap)

    wide = pltpu.VMEM((width, pairs * width), F32)
    whole = pltpu.VMEM((width, width), BF16)
    halfway = pltpu.VMEM((pairs * width, width), BF16)
    acc = call(ladder_first, wide, [VMEM] * 2, [halfway], flops=2 * flops, moved=moved)(r, own)

    packed = call(pack, pltpu.VMEM((quarter + fold, width), BF16), [VMEM] * 3)(part, got, piece)
    other = lax.ppermute(packed, ("grp", "ja"), chip_swap)
    packed = call(
        functools.partial(repack, quarter), pltpu.VMEM((2 * quarter + fold, width), BF16), [VMEM] * 2
    )(packed, other)
    apart = 4
    while apart < n_j:
        more = lax.ppermute(packed[2 * quarter :], "ja", [(j, j ^ apart) for j in range(n_j)])
        more = (packed[2 * quarter :].astype(F32) + more.astype(F32)).astype(BF16)
        packed = jnp.concatenate([packed[: 2 * quarter], more], 0)
        apart *= 2
    other = lax.ppermute(packed, "ja", core_swap)

    swapped = {}
    for k, mine in near.items():
        swapped[k] = lax.ppermute(mine, "ja", core_swap)
    *before, last = near
    for k in before:
        acc = call(
            functools.partial(ladder_near, spot),
            wide,
            [VMEM] * 4,
            [whole, halfway],
            {0: 0},
            flops=2 * flops,
            moved=moved,
        )(acc, r, near[k], swapped[k])
    ahead = call(
        functools.partial(ladder_ahead, spot, quarter),
        pltpu.VMEM((2 * half, pairs * width), BF16),
        [VMEM] * 3,
        flops=flops,
        moved=moved,
    )(r, packed, near[last])
    out = call(
        functools.partial(ladder_last, spot, first_j, quarter),
        jax.ShapeDtypeStruct((pairs, width, width), BF16),
        [VMEM] * 8,
        [
            pltpu.VMEM((pairs * width, 2 * width), BF16),
            pltpu.VMEM((width, 2 * width), BF16),
            pltpu.VMEM((width, rank), BF16),
            pltpu.VMEM((pairs, width, width), BF16),
            pltpu.SemaphoreType.DMA((pairs,)),
        ],
        flops=3 * flops,
        moved=2 * moved,
    )(acc, r, packed, other, near[last], swapped[last], cycle_factors, ahead)
    return out.reshape(doubles.shape)


def solution(mesh):
    n_g, n_i, n_j = (mesh.shape[axis] for axis in ("grp", "ia", "ja"))
    in_specs = (P(("grp", "ia"), "ja", None, None), P("ia", None, None), P())
    out_specs = P(("grp", "ia"), "ja", None, None)

    def block(*args):
        return sigma_block(n_g, n_i, n_j, *args)

    return jax.shard_map(block, mesh=mesh, in_specs=in_specs, out_specs=out_specs, check_vma=False)
```

```python
import functools

import jax
import jax.numpy as jnp
from jax import lax
from jax.experimental import pallas as pl
from jax.experimental.pallas import tpu as pltpu
from jax.sharding import PartitionSpec as P

F32 = jnp.float32
BF16 = jnp.bfloat16
NT = (((1,), (1,)), ((), ()))
VMEM = pl.BlockSpec(memory_space=pltpu.VMEM)
HBM = pl.BlockSpec(memory_space=pltpu.HBM)


def call(kernel, outs, specs, scratch=(), aliases=None, flops=0, moved=0):
    return pl.pallas_call(
        kernel,
        out_shape=outs,
        in_specs=specs,
        out_specs=jax.tree.map(lambda o: VMEM if isinstance(o, pl.MemoryRef) else HBM, outs),
        scratch_shapes=scratch,
        input_output_aliases=aliases or {},
        cost_estimate=pl.CostEstimate(flops=flops, bytes_accessed=moved, transcendentals=0),
        compiler_params=pltpu.CompilerParams(vmem_limit_bytes=24 << 20),
    )


def in_hbm(x):
    return pltpu.with_memory_space_constraint(x, pltpu.HBM)


def mm(a, b):
    return jnp.dot(a, b, preferred_element_type=F32)


def mm_nt(a, b):
    return lax.dot_general(a, b, NT, preferred_element_type=F32)


def take_far(index_of, src, out, sems):
    count = sems.shape[0]
    rows = out.shape[0] // count
    copies = []
    for k in range(count):
        at = pl.multiple_of((index_of() * count + k) * rows, rows)
        copies.append(pltpu.make_async_copy(src.at[pl.ds(at, rows), :], out.at[pl.ds(k * rows, rows), :], sems.at[k]))
        copies[-1].start()
    for copy in copies:
        copy.wait()


def take_near(core_of, src, ours, theirs):
    rows = ours.shape[0]
    for out, index in ((ours, core_of()), (theirs, 1 - core_of())):
        out[...] = src[pl.ds(pl.multiple_of(index * rows, rows), rows), :]


def latent_part(first_j, r, u, out):
    j = first_j()
    acc = mm(r[0], u[j])
    for q in range(1, r.shape[0]):
        acc = acc + mm(r[q], u[j + q])
    out[...] = acc


def ladder_sum(r, factors, halfway):
    n, width, _ = r.shape
    rows = r[...].reshape(n * width, width)
    for p, b in enumerate(factors):
        h = mm_nt(b, rows).astype(BF16)
        for q in range(n):
            halfway[q * width : (q + 1) * width, p * width : (p + 1) * width] = h[:, q * width : (q + 1) * width]
    wide = factors[0] if len(factors) == 1 else jnp.concatenate(factors, 1)
    return mm_nt(wide, halfway[...])


def ladder_first(r, b, out, halfway):
    out[...] = ladder_sum(r, [b[...]], halfway)


def join(core, mine, theirs, whole):
    rows = mine.shape[0]
    whole[pl.ds(pl.multiple_of(core * rows, rows), rows), :] = mine[...]
    whole[pl.ds(pl.multiple_of((1 - core) * rows, rows), rows), :] = theirs[...]


def ladder_near(spot, acc, r, mine, theirs, out, whole, halfway):
    join(spot()[1], mine, theirs, whole)
    out[...] = acc[...] + ladder_sum(r, [whole[...]], halfway)


def pack(part, got, piece, out):
    rows, width = piece.shape
    rank = part.shape[1]
    out[:rows] = piece[...]
    total = (part[...] + got[...]).astype(BF16)
    deep = out.shape[0] - rows
    for k in range(width // rank):
        out[rows:, k * rank : (k + 1) * rank] = total[k * deep : (k + 1) * deep]


def repack(rows, mine, theirs, out):
    out[:rows] = mine[:rows]
    out[rows : 2 * rows] = theirs[:rows]
    out[2 * rows :] = (mine[rows:].astype(F32) + theirs[rows:].astype(F32)).astype(BF16)


def first_products(r, pieces, halfway):
    n, width, _ = r.shape
    stack = jnp.concatenate([rows for rows, _, _ in pieces], 0)
    for g in range(0, n, 2):
        h = mm_nt(stack, r[g : g + 2].reshape(2 * width, width)).astype(BF16)
        top = 0
        for rows, p, start in pieces:
            size = rows.shape[0]
            for k in range(2):
                at = pl.multiple_of((g + k) * width + start, size)
                halfway[pl.ds(at, size), p * width : (p + 1) * width] = h[top : top + size, k * width : (k + 1) * width]
            top += size


def held_rows(spot, rows, which, packed, near):
    parity, _ = spot()
    half = near.shape[0]
    return [
        (packed[:rows], 0, (parity * 2 + which) * rows),
        (packed[rows : 2 * rows], 0, ((1 - parity) * 2 + which) * rows),
        (near[...], 1, which * half),
    ]


def ladder_ahead(spot, rows, r, packed, near, halfway):
    first_products(r, held_rows(spot, rows, spot()[1], packed, near), halfway)


def ladder_last(
    spot, first_j, rows, acc, r, packed, other, near, swapped, u, ahead, out, halfway, wide, latent, held, sems
):
    n, width, _ = r.shape
    core = spot()[1]
    theirs = held_rows(spot, rows, 1 - core, other, swapped)
    first_products(r, theirs, halfway)
    for piece, p, start in held_rows(spot, rows, core, packed, near) + theirs:
        size = piece.shape[0]
        wide[pl.ds(pl.multiple_of(start, size), size), p * width : (p + 1) * width] = piece
    folded = jnp.where(core == 0, packed[2 * rows :], other[2 * rows :])
    deep, rank = folded.shape[0], latent.shape[1]
    for k in range(width // rank):
        latent[k * deep : (k + 1) * deep] = folded[:, k * rank : (k + 1) * rank]
    j = first_j()
    copies = []
    for g in range(0, n, 2):
        span = slice(g * width, (g + 2) * width)
        term = mm_nt(wide[...], halfway[span])
        cycle = mm_nt(latent[...], u[pl.ds(j + g, 2)].reshape(2 * width, rank)).astype(BF16)
        total = (acc[:, span] + term + cycle.astype(F32)).astype(BF16)
        for k in range(2):
            held[g + k] = total[:, k * width : (k + 1) * width]
            copies.append(pltpu.make_async_copy(held.at[g + k], out.at[g + k], sems.at[g + k]))
            copies[-1].start()
    for copy in copies:
        copy.wait()


def sigma_block(n_g, n_i, n_j, doubles, aux_factors, cycle_factors):
    rows_i, cols_j, width, _ = doubles.shape
    pairs = rows_i * cols_j
    rank = cycle_factors.shape[-1]
    r = doubles.reshape(pairs, width, width)
    own = aux_factors.reshape(width, width)
    quarter, half = width // 4, width // 2
    fold = rank
    assert width % rank == 0 and pairs % 2 == 0 and n_g % 2 == 0 and n_j % 4 == 0
    flops = 2 * pairs * width * width * width
    moved = 2 * pairs * width * width

    def spot():
        j = lax.axis_index("ja")
        return lax.rem(lax.div(j, 2) + lax.axis_index("grp"), 2), lax.rem(j, 2)

    def first_j():
        return lax.axis_index("ja") * cols_j

    def quarter_of():
        parity, core = spot()
        return parity * 2 + 1 - core

    def across(i, k):
        return i ^ k if n_i & (n_i - 1) == 0 else (i + k) % n_i

    def over(k):
        return [(i * n_j + j, across(i, k) * n_j + (j ^ 1)) for i in range(n_i) for j in range(n_j)]

    core_swap = [(j, j ^ 1) for j in range(n_j)]
    chip_swap = [
        (g * n_j + j, (g ^ 1) * n_j + j if j % 2 else g * n_j + (j ^ 2)) for g in range(n_g) for j in range(n_j)
    ]
    far_away = n_i // 2

    piece = call(
        functools.partial(take_far, quarter_of),
        pltpu.VMEM((quarter, width), BF16),
        [HBM],
        [pltpu.SemaphoreType.DMA((3 if quarter % 48 == 0 else 1,))],
        flops=2 * flops,
        moved=moved * 2 // 2,
    )(in_hbm(own))
    piece = lax.ppermute(piece, ("ia", "ja"), over(far_away))
    rows, other_rows = call(
        functools.partial(take_near, lambda: spot()[1]),
        (pltpu.VMEM((half, width), BF16), pltpu.VMEM((half, width), BF16)),
        [VMEM],
        flops=16 * flops,
        moved=8 * moved,
    )(own)
    near = {}
    for k in range(1, n_i):
        if k != far_away:
            if k == 1:
                near[k] = lax.ppermute(rows, "ia", [(i, across(i, k)) for i in range(n_i)])
            else:
                near[k] = lax.ppermute(other_rows, ("ia", "ja"), over(k))

    part = call(
        functools.partial(latent_part, first_j),
        pltpu.VMEM((width, rank), F32),
        [VMEM] * 2,
        flops=flops * rank // width,
        moved=moved,
    )(r, cycle_factors)
    got = lax.ppermute(part, "ja", core_swap)

    wide = pltpu.VMEM((width, pairs * width), F32)
    whole = pltpu.VMEM((width, width), BF16)
    halfway = pltpu.VMEM((pairs * width, width), BF16)
    acc = call(ladder_first, wide, [VMEM] * 2, [halfway], flops=2 * flops, moved=moved)(r, own)

    packed = call(pack, pltpu.VMEM((quarter + fold, width), BF16), [VMEM] * 3)(part, got, piece)
    other = lax.ppermute(packed, ("grp", "ja"), chip_swap)
    packed = call(
        functools.partial(repack, quarter), pltpu.VMEM((2 * quarter + fold, width), BF16), [VMEM] * 2
    )(packed, other)
    apart = 4
    while apart < n_j:
        more = lax.ppermute(packed[2 * quarter :], "ja", [(j, j ^ apart) for j in range(n_j)])
        more = (packed[2 * quarter :].astype(F32) + more.astype(F32)).astype(BF16)
        packed = jnp.concatenate([packed[: 2 * quarter], more], 0)
        apart *= 2
    other = lax.ppermute(packed, "ja", core_swap)

    swapped = {}
    for k, mine in near.items():
        swapped[k] = lax.ppermute(mine, "ja", core_swap)
    *before, last = near
    for k in before:
        acc = call(
            functools.partial(ladder_near, spot),
            wide,
            [VMEM] * 4,
            [whole, halfway],
            {0: 0},
            flops=2 * flops,
            moved=moved,
        )(acc, r, near[k], swapped[k])
    ahead = call(
        functools.partial(ladder_ahead, spot, quarter),
        pltpu.VMEM((pairs * width, 2 * width), BF16),
        [VMEM] * 3,
        flops=flops,
        moved=moved,
    )(r, packed, near[last])
    out, _ = call(
        functools.partial(ladder_last, spot, first_j, quarter),
        (jax.ShapeDtypeStruct((pairs, width, width), BF16), pltpu.VMEM((pairs * width, 2 * width), BF16)),
        [VMEM] * 8,
        [
            pltpu.VMEM((width, 2 * width), BF16),
            pltpu.VMEM((width, rank), BF16),
            pltpu.VMEM((pairs, width, width), BF16),
            pltpu.SemaphoreType.DMA((pairs,)),
        ],
        {7: 1},
        flops=3 * flops,
        moved=2 * moved,
    )(acc, r, packed, other, near[last], swapped[last], cycle_factors, ahead)
    return out.reshape(doubles.shape)


def solution(mesh):
    n_g, n_i, n_j = (mesh.shape[axis] for axis in ("grp", "ia", "ja"))
    in_specs = (P(("grp", "ia"), "ja", None, None), P("ia", None, None), P())
    out_specs = P(("grp", "ia"), "ja", None, None)

    def block(*args):
        return sigma_block(n_g, n_i, n_j, *args)

    return jax.shard_map(block, mesh=mesh, in_specs=in_specs, out_specs=out_specs, check_vma=False)
```
